32 devices in a mesh: expert: 16 (over z, y, x), replica: 2 (over core).
Axes of the slice: x: 2, y: 2, z: 4, core: 2. Of those that a mesh axis runs over, the one named last changes fastest.
Arguments:
- samples: float32 [32768, 256], P(('expert', 'replica')), may hold values from -6 to 6
- routes: int32 [32768, 1], P(('expert', 'replica')), may hold values from 0 to 15; in each aligned block of 1024 rows (0 to 1023, 1024 to 2047, ...) at most 128 rows name the same one
- cotangent: float32 [32768, 256], P(('expert', 'replica')), may hold values from -6 to 6
- weights: float32 [7, 16, 256, 256], P(None, 'expert', 'replica'), may hold values from -0.375 to 0.375
- moment_one: float32 [7, 16, 256, 256], P(None, 'expert', 'replica'), may hold values from -6 to 6
- moment_two: float32 [7, 16, 256, 256], P(None, 'expert', 'replica'), may hold values from 1 to 30
Outputs:
- outputs: float32 [32768, 256], P(('expert', 'replica'))
- new_weights: float32 [7, 16, 256, 256], P(None, 'expert', 'replica')
- new_moment_one: float32 [7, 16, 256, 256], P(None, 'expert', 'replica')
- new_moment_two: float32 [7, 16, 256, 256], P(None, 'expert', 'replica')
The draws below stay inside these ranges and needn't reach their ends.
Inputs may be any that keep to these rules, and one draw needn't show every extreme that they name: `routes`: among the 1024 rows of one device no expert is chosen by more than 128 rows; some expert is chosen by exactly 128 rows of some device.
All inputs are finite; a program needn't handle non-finite values.
Results may differ from the reference program's by a relative error of at most 0.0002.
Values sent between devices are 32-bit elements; how exact they have to be, the bound alone decides.
No kernel may reach another device: no remote copies, remote signals or barrier semaphores. Data moves between devices by JAX's collectives and lax.ppermute only.
A program may use at most 128 MiB of HBM per device.

```python
import math
import jax
import jax.numpy as jnp
import numpy as np
from jax import lax

D = 256
LAYERS = 7
TOK_DEV = 1024
EXPERTS = 16
CAP = 128
ROWS = 32768
DEVICES = 32


def block_levels(stream_key, extent, pieces, low, largest):
    factor_of = 1.0
    for axis_at, blocks in pieces:
        steps = jax.random.uniform(jax.random.fold_in(jax.random.fold_in(stream_key, 6), axis_at), (blocks,), jnp.float32, low / len(pieces), largest / len(pieces))
        factor_of = factor_of * jnp.repeat(jnp.exp(steps), extent[axis_at] // blocks).reshape((-1,) + (1,) * (len(extent) - 1 - axis_at))
    return factor_of


def routed_block(stream_key, own, number, rows, count, top, bound, lean):
    sequence = jax.random.permutation(stream_key, count)
    crowded, usual = load_shares(count, rows * top, bound, lean, True), load_shares(count, rows * top, bound, lean, False)
    places = jnp.arange(count)

    def named(tallies, turn):
        used = int((tallies > 0).sum())
        fixed = max(1, used // 4)
        shifted = fixed + (places - fixed + turn * (used - fixed)) % max(1, count - fixed)
        return jnp.zeros((count,), jnp.int32).at[sequence[jnp.where(places < fixed, places, shifted)]].set(jnp.asarray(tallies, jnp.int32))

    tallies = jnp.where(number % 4 == 0, named(crowded, number // 4), named(usual, number - number // 4 - 1))
    mixed = jax.random.permutation(jax.random.fold_in(own, 3), count)
    giver, receiver = mixed[0:count // 2 * 2:2], mixed[1:count // 2 * 2:2]
    slack = jnp.minimum(tallies[giver] - 1, bound - tallies[receiver]) // 2
    slack = jnp.where((giver == sequence[0]) | (receiver == sequence[0]) | (tallies[receiver] == 0), 0, jnp.maximum(slack, 0))
    shifted = jax.random.randint(jax.random.fold_in(own, 4), (count // 2,), 0, 1 << 20) % (slack + 1)
    tallies = tallies.at[giver].add(-shifted).at[receiver].add(shifted)
    items = jnp.searchsorted(jnp.cumsum(tallies), jnp.arange(rows * top), side="right").astype(jnp.int32)
    listing = items.reshape(top, rows).T
    listing = listing[jax.random.permutation(jax.random.fold_in(own, 1), rows)]
    turn = jax.random.randint(jax.random.fold_in(own, 2), (rows, 1), 0, top)
    return jnp.take_along_axis(listing, (jnp.arange(top)[None, :] + turn) % top, axis=1)


def load_shares(count, total, reach, skew, full):
    loads = [(1 << 20) // math.isqrt(grade ** skew) + 1 for grade in range(1, count + 1)]
    largest = reach if full else min(reach, max(-(-total // count), total * loads[0] // sum(loads)))
    least = 1 if total - largest >= count - 1 else 0
    given, spare = [largest] + [least] * (count - 1), total - largest - least * (count - 1)
    while spare > 0:
        candidates = [i for i in range(1, count) if given[i] < largest] or [i for i in range(1, count) if given[i] < reach]
        pool, remaining = sum([loads[i] for i in candidates]), spare
        for i in candidates:
            more = min(reach - given[i], max(1, remaining * loads[i] // pool), spare)
            given[i] = given[i] + more
            spare = spare - more
    return np.array(given)


def normal_values(stream_key, dims, scale, limit, pieces=(), kind=jnp.bfloat16):
    entries = scale * jax.random.normal(stream_key, dims, jnp.float32)
    if pieces:
        entries = entries * block_levels(stream_key, dims, pieces, -0.22, 0.18)
    return jnp.clip(entries, -limit, limit).astype(kind)


def setup_inputs(seed: int = 0) -> dict:
    keys = jax.random.split(jax.random.key(seed), 7)
    samples = normal_values(keys[0], (ROWS, D), 1.0, 6.0, ((0, 32),), jnp.float32)
    routes_keys = jax.random.split(jax.random.fold_in(keys[1], 1), ROWS // TOK_DEV)
    routes_turns = jax.random.permutation(jax.random.fold_in(keys[1], 3), ROWS // TOK_DEV)
    routes = jax.vmap(lambda own, number: routed_block(jax.random.fold_in(keys[1], 2), own, number, TOK_DEV, EXPERTS, 1, CAP, 2))(routes_keys, routes_turns).reshape((ROWS, 1))
    cotangent = normal_values(keys[2], (ROWS, D), 1.0, 6.0, ((0, 32),), jnp.float32)
    weights = normal_values(keys[3], (LAYERS, EXPERTS, D, D), D ** -0.5, 0.375, ((1, 16), (2, 2)), jnp.float32)
    moment_one = normal_values(keys[4], (LAYERS, EXPERTS, D, D), 1.0, 6.0, ((1, 16), (2, 2)), jnp.float32)
    moment_two = jnp.clip(jnp.exp(math.log(30.0) - 3.4011974 * jax.random.uniform(keys[5], (LAYERS, EXPERTS, D, D), jnp.float32) ** block_levels(keys[5], (LAYERS, EXPERTS, D, D), ((1, 16), (2, 2)), -0.2, 0.2)), 1.0, 30.0)
    return {"samples": samples, "routes": routes, "cotangent": cotangent, "weights": weights, "moment_one": moment_one, "moment_two": moment_two}


HIGH = lax.Precision.HIGHEST
CORR_ONE = 0.9999734386011124
CORR_TWO = 0.09520785288629038

def silu_slope(value):
    sigma = jax.nn.sigmoid(value)
    return sigma * (1.0 + value * (1.0 - sigma))

def expert_pass(inputs):
    rows, grads_in, mats = inputs
    acts = []
    pres = []
    hidden = rows
    for layer in range(LAYERS):
        acts.append(hidden)
        pre = jnp.dot(hidden, mats[layer], precision=HIGH, preferred_element_type=jnp.float32)
        pres.append(pre)
        if layer < LAYERS - 1:
            hidden = pre * jax.nn.sigmoid(pre)
    delta = grads_in
    grads = [None] * LAYERS
    for layer in range(LAYERS - 1, -1, -1):
        grads[layer] = lax.dot_general(acts[layer], delta, (((0,), (0,)), ((), ())), precision=HIGH, preferred_element_type=jnp.float32)
        if layer > 0:
            back = lax.dot_general(delta, mats[layer], (((1,), (1,)), ((), ())), precision=HIGH, preferred_element_type=jnp.float32)
            delta = back * silu_slope(pres[layer - 1])
    return (pres[LAYERS - 1], jnp.stack(grads))

def reference(samples, routes, cotangent, weights, moment_one, moment_two):
    route = routes[:, 0].astype(jnp.int32)
    blocked = route.reshape(DEVICES, TOK_DEV)
    onehot = (blocked[:, :, None] == jnp.arange(EXPERTS, dtype=jnp.int32)[None, None, :]).astype(jnp.int32)
    before = jnp.cumsum(onehot, axis=1) - onehot
    rank = lax.optimization_barrier(jnp.sum(before * onehot, axis=2)).reshape(-1)
    source = (jnp.arange(DEVICES * TOK_DEV, dtype=jnp.int32) // TOK_DEV).astype(jnp.int32)
    slot = route * (DEVICES * CAP) + source * CAP + rank
    total = EXPERTS * DEVICES * CAP
    packed = jnp.zeros((total, D), jnp.float32).at[slot].set(samples).reshape(EXPERTS, DEVICES * CAP, D)
    packed_cot = jnp.zeros((total, D), jnp.float32).at[slot].set(cotangent).reshape(EXPERTS, DEVICES * CAP, D)
    mats = jnp.transpose(weights, (1, 0, 2, 3))
    results, grads = lax.map(expert_pass, (packed, packed_cot, mats))
    outputs = results.reshape(total, D)[slot]
    grad = jnp.transpose(grads, (1, 0, 2, 3))
    new_one = 0.9 * moment_one + 0.1 * grad
    new_two = 0.999 * moment_two + 0.001 * grad * grad
    new_w = weights - 0.01 * (new_one / CORR_ONE) / (jnp.sqrt(new_two / CORR_TWO) + 1e-08)
    return (outputs, new_w, new_one, new_two)
```

```python
import functools

import jax
import jax.numpy as jnp
from jax import lax
from jax.experimental import pallas as pl
from jax.experimental.pallas import tpu as pltpu
from jax.sharding import PartitionSpec as P

CORR_ONE = 0.9999734386011124
CORR_TWO = 0.09520785288629038
PLANES = 4

F32 = jnp.float32
BF16 = jnp.bfloat16


def split(value):
    high = value.astype(BF16)
    return high, (value - high.astype(F32)).astype(BF16)


def dot(a, b, dims):
    return lax.dot_general(a, b, (dims, ((), ())), preferred_element_type=F32)


def dot3(ah, al, bh, bl, dims):
    return dot(ah, bh, dims) + (dot(ah, bl, dims) + dot(al, bh, dims))


NN = ((1,), (0,))
NT = ((1,), (1,))
TN = ((0,), (0,))


def slots_of(route, rank, plane, column, size, cap):
    own = jnp.right_shift(route, size.bit_length() - 1)
    chip = jnp.bitwise_and(route, size - 1)
    near = jnp.bitwise_xor(own, plane)
    inner = jnp.bitwise_and(jnp.bitwise_xor(jnp.right_shift(own, 1), own), 1)
    step = jnp.where(near < 2, near, 3 - inner)
    mask = jnp.bitwise_xor(chip, column)
    return (step * size + mask) * cap + rank


def position(size):
    at = lax.axis_index("expert")
    return jnp.right_shift(at, size.bit_length() - 1), jnp.bitwise_and(at, size - 1)


def pack_body(size, cap, groups, route_ref, rows_ref, *outs):
    count = rows_ref.shape[0]
    plane, column = position(size)
    route = route_ref[...]
    hot = (lax.broadcasted_iota(jnp.int32, (groups, count), 0) == route).astype(F32)
    ahead = (
        lax.broadcasted_iota(jnp.int32, (count, count), 0)
        < lax.broadcasted_iota(jnp.int32, (count, count), 1)
    ).astype(F32).astype(BF16)
    before = dot(hot.astype(BF16), ahead, NN)
    rank = jnp.sum(before * hot, axis=0, keepdims=True).astype(jnp.int32)
    slot = slots_of(route, rank, plane, column, size, cap)
    high, low = split(rows_ref[...])
    half = 2 * size * cap
    for part in range(2):
        pick = (
            lax.broadcasted_iota(jnp.int32, (half, count), 0) + part * half == slot
        ).astype(F32).astype(BF16)
        rows = dot(pick, high, NN) + dot(pick, low, NN)
        for mask in range(size):
            out = outs[part * size + mask]
            for step in range(2):
                at = (step * size + mask) * cap
                out[step] = rows[at : at + cap]


def pack(route_row, rows, size, cap, groups):
    count, width = rows.shape
    return pl.pallas_call(
        functools.partial(pack_body, size, cap, groups),
        out_shape=[jax.ShapeDtypeStruct((2, cap, width), F32)] * (2 * size),
        compiler_params=pltpu.CompilerParams(vmem_limit_bytes=48 * 2**20),
        cost_estimate=pl.CostEstimate(
            flops=8 * count * count * width, bytes_accessed=12 * count * width, transcendentals=0
        ),
        name="pack",
    )(route_row, rows)


def unpack_body(size, cap, groups, route_ref, *refs):
    out_ref = refs[-1]
    count = out_ref.shape[0]
    plane, column = position(size)
    route = route_ref[...]
    hot = (lax.broadcasted_iota(jnp.int32, (count, groups), 1) == route).astype(F32)
    ahead = (
        lax.broadcasted_iota(jnp.int32, (count, count), 1)
        < lax.broadcasted_iota(jnp.int32, (count, count), 0)
    ).astype(F32).astype(BF16)
    before = dot(ahead, hot.astype(BF16), NN)
    rank = jnp.sum(before * hot, axis=1, keepdims=True).astype(jnp.int32)
    slot = slots_of(route, rank, plane, column, size, cap)
    total = None
    for step in range(PLANES):
        rows = jnp.concatenate([refs[step * size + m][...] for m in range(size)], axis=0)
        high, low = split(rows)
        at = lax.broadcasted_iota(jnp.int32, (count, size * cap), 1) + step * size * cap
        pick = (at == slot).astype(F32).astype(BF16)
        term = dot(pick, high, NN) + dot(pick, low, NN)
        total = term if total is None else total + term
    out_ref[...] = total


def unpack(route_col, pieces, size, cap, groups):
    count = route_col.shape[0]
    width = pieces[0].shape[-1]
    return pl.pallas_call(
        functools.partial(unpack_body, size, cap, groups),
        out_shape=jax.ShapeDtypeStruct((count, width), F32),
        compiler_params=pltpu.CompilerParams(vmem_limit_bytes=48 * 2**20),
        cost_estimate=pl.CostEstimate(
            flops=8 * count * count * width, bytes_accessed=12 * count * width, transcendentals=0
        ),
        name="unpack",
    )(route_col, *pieces)


def step_body(size, cap, layers, chunks, *refs):
    rows_in = refs[:size]
    cots_in = refs[size : 2 * size]
    mine, other = refs[2 * size : 2 * size + 2]
    at = 2 * size + 2
    outs = refs[at : at + size]
    at += size
    keeps = refs[at : at + len(chunks)]
    sends = refs[at + len(chunks) : at + 2 * len(chunks)]
    at += 2 * len(chunks)
    wh, wl, ah, al, slope, full = refs[at:]
    width = full.shape[0]
    shard = mine.shape[1]
    core = lax.axis_index("replica")
    here = pl.multiple_of(core * shard, shard)
    there = pl.multiple_of(width - shard - core * shard, shard)

    for m in range(size):
        high, low = split(rows_in[m][0])
        ah[0, m * cap : (m + 1) * cap] = high
        al[0, m * cap : (m + 1) * cap] = low

    def weights(layer):
        high, low = split(mine[layer])
        wh[layer, pl.ds(here, shard)] = high
        wl[layer, pl.ds(here, shard)] = low
        high, low = split(other[layer])
        wh[layer, pl.ds(there, shard)] = high
        wl[layer, pl.ds(there, shard)] = low

    def forward(layer, _):
        weights(layer)
        pre = dot3(ah[layer], al[layer], wh[layer], wl[layer], NN)
        sigma = jax.nn.sigmoid(pre)
        high, low = split(pre * sigma)
        ah[layer + 1] = high
        al[layer + 1] = low
        slope[layer] = sigma * (1.0 + pre * (1.0 - sigma))
        return 0

    lax.fori_loop(0, layers - 1, forward, 0)
    last = layers - 1
    weights(last)
    result = dot3(ah[last], al[last], wh[last], wl[last], NN)
    for m in range(size):
        outs[m][...] = result[m * cap : (m + 1) * cap]

    delta = jnp.concatenate([cots_in[m][0] for m in range(size)], axis=0)
    dh, dl = split(delta)
    for keep, send, chunk in zip(keeps, sends, chunks):
        for layer in chunk:
            place = layer - min(chunk)
            full[...] = dot3(ah[layer], al[layer], dh, dl, TN)
            keep[place] = full[pl.ds(here, shard)]
            send[place] = full[pl.ds(there, shard)]
            if layer > 0:
                back = dot3(dh, dl, wh[layer], wl[layer], NT)
                dh, dl = split(back * slope[layer - 1])


def step_call(rows, cots, mine, other, which, chunks):
    size = len(rows)
    cap, width = rows[0].shape[1:]
    layers, shard = mine.shape[:2]
    items = size * cap
    row_spec = pl.BlockSpec((1, cap, width), lambda i: (which, 0, 0))
    weight_spec = pl.BlockSpec((layers, shard, width), lambda i: (0, 0, 0))
    outs = [jax.ShapeDtypeStruct((cap, width), F32)] * size
    out_specs = [pl.BlockSpec((cap, width), lambda i: (0, 0))] * size
    grads = [jax.ShapeDtypeStruct((len(c), shard, width), F32) for c in chunks] * 2
    grad_specs = [pl.BlockSpec((len(c), shard, width), lambda i: (0, 0, 0)) for c in chunks] * 2
    result = pl.pallas_call(
        functools.partial(step_body, size, cap, layers, chunks),
        grid=(1,),
        in_specs=[row_spec] * (2 * size) + [weight_spec] * 2,
        out_specs=out_specs + grad_specs,
        out_shape=outs + grads,
        scratch_shapes=[
            pltpu.VMEM((layers, width, width), BF16),
            pltpu.VMEM((layers, width, width), BF16),
            pltpu.VMEM((layers, items, width), BF16),
            pltpu.VMEM((layers, items, width), BF16),
            pltpu.VMEM((layers - 1, items, width), F32),
            pltpu.VMEM((width, width), F32),
        ],
        compiler_params=pltpu.CompilerParams(vmem_limit_bytes=48 * 2**20),
        cost_estimate=pl.CostEstimate(
            flops=18 * layers * items * width * width,
            bytes_accessed=4 * (3 * items * width + 2 * layers * width * width),
            transcendentals=layers * items * width,
        ),
        name="step",
    )(*rows, *cots, mine, other)
    n = len(chunks)
    return result[:size], result[size : size + n], result[size + n :]


def on_device(samples, routes, cotangent, weights, moment_one, moment_two):
    count = samples.shape[0]
    groups = lax.axis_size("expert")
    cap = 2 * count // groups
    size = groups // PLANES
    layers = weights.shape[0]
    route_row = routes.reshape(1, count)

    def plane_pairs(pairs):
        return [(a * size + p, b * size + p) for a, b in pairs for p in range(size)]

    def along(value, pairs):
        return lax.ppermute(value, "expert", plane_pairs(pairs))

    def swap_core(value):
        return lax.ppermute(value, "replica", [(0, 1), (1, 0)])

    def to_mask(value, mask):
        if mask == 0:
            return value
        return lax.ppermute(value, "expert", [(e, e ^ mask) for e in range(groups)])

    SIDES = [(0, 1), (1, 0), (2, 3), (3, 2)]
    MIDDLE = [(1, 2), (2, 1)]
    OUTWARD = [(1, 0), (2, 3)]
    INWARD = [(0, 1), (3, 2)]

    own = weights[:, 0]
    side = along(own, SIDES)
    middle = along(own, MIDDLE)
    own_other = swap_core(own)

    packed = pack(route_row, samples, size, cap, groups)
    arrived = [to_mask(value, i % size) for i, value in enumerate(packed)]
    packed_cot = pack(route_row, cotangent, size, cap, groups)
    arrived_cot = [to_mask(value, i % size) for i, value in enumerate(packed_cot)]

    middle_out = along(middle, OUTWARD)
    side_in = along(side, MIDDLE)
    side_out = along(side_in, OUTWARD)
    side_other = swap_core(side)
    second = middle + middle_out
    third = side_in + side_out
    mats = [
        (own, own_other),
        (side, side_other),
        (second, swap_core(second)),
        (third, swap_core(third)),
    ]
    whole = [list(range(layers - 1, -1, -1))]
    fine = [[6, 5], [4, 3], [2, 1, 0]] if layers == 7 else whole
    outputs = []
    sums = []
    for step in range(PLANES):
        part = step // 2
        outs, keeps, sends = step_call(
            arrived[part * size : (part + 1) * size],
            arrived_cot[part * size : (part + 1) * size],
            *mats[step],
            step % 2,
            fine,
        )
        outputs += [to_mask(value, m) for m, value in enumerate(outs)]
        sums.append([keep + swap_core(send) for keep, send in zip(keeps, sends)])

    pieces = []
    for j in range(len(fine)):
        zero, one, two, three = (s[j] for s in sums)
        first_in = along(one, INWARD)
        second_in = two + along(two, INWARD)
        second_mid = along(second_in, MIDDLE)
        third_in = three + along(three, INWARD)
        third_mid = one + along(third_in, MIDDLE)
        third_out = along(third_mid, OUTWARD)
        pieces.append(zero + first_in + second_mid + third_out)
    grad = jnp.concatenate(pieces[::-1], axis=0)[:, None]
    new_one = 0.9 * moment_one + 0.1 * grad
    new_two = 0.999 * moment_two + 0.001 * grad * grad
    new_w = weights - 0.01 * (new_one / CORR_ONE) / (jnp.sqrt(new_two / CORR_TWO) + 1e-08)
    result = unpack(routes, outputs, size, cap, groups)
    return (result, new_w, new_one, new_two)


def solution(mesh):
    placed = (
        P(("expert", "replica"), None),
        P(("expert", "replica"), None),
        P(("expert", "replica"), None),
        P(None, "expert", "replica", None),
        P(None, "expert", "replica", None),
        P(None, "expert", "replica", None),
    )
    return jax.shard_map(
        on_device,
        mesh=mesh,
        in_specs=placed,
        out_specs=(
            P(("expert", "replica"), None),
            P(None, "expert", "replica", None),
            P(None, "expert", "replica", None),
            P(None, "expert", "replica", None),
        ),
        check_vma=False,
    )
```

```python
import functools

import jax
import jax.numpy as jnp
from jax import lax
from jax.experimental import pallas as pl
from jax.experimental.pallas import tpu as pltpu
from jax.sharding import PartitionSpec as P


CORR_ONE = 0.9999734386011124
CORR_TWO = 0.09520785288629038
PLANES = 4

F32 = jnp.float32
BF16 = jnp.bfloat16


def split(value):
    high = value.astype(BF16)
    return high, (value - high.astype(F32)).astype(BF16)


def dot(a, b, dims):
    return lax.dot_general(a, b, (dims, ((), ())), preferred_element_type=F32)


def dot3(ah, al, bh, bl, dims):
    return dot(ah, bh, dims) + (dot(ah, bl, dims) + dot(al, bh, dims))


NN = ((1,), (0,))
NT = ((1,), (1,))
TN = ((0,), (0,))


def slots_of(route, rank, plane, column, size, cap):
    own = jnp.right_shift(route, size.bit_length() - 1)
    chip = jnp.bitwise_and(route, size - 1)
    near = jnp.bitwise_xor(own, plane)
    inner = jnp.bitwise_and(jnp.bitwise_xor(jnp.right_shift(own, 1), own), 1)
    step = jnp.where(near < 2, near, 3 - inner)
    mask = jnp.bitwise_xor(chip, column)
    return (step * size + mask) * cap + rank


def position(size):
    at = lax.axis_index("expert")
    return jnp.right_shift(at, size.bit_length() - 1), jnp.bitwise_and(at, size - 1)


def pack_body(size, cap, groups, steps, route_ref, rows_ref, cots_ref, *outs):
    count, _ = rows_ref.shape
    plane, column = position(size)
    route = route_ref[...]
    hot = (lax.broadcasted_iota(jnp.int32, (groups, count), 0) == route).astype(F32)
    ahead = (
        lax.broadcasted_iota(jnp.int32, (count, count), 0)
        < lax.broadcasted_iota(jnp.int32, (count, count), 1)
    ).astype(F32).astype(BF16)
    before = dot(hot.astype(BF16), ahead, NN)
    rank = jnp.sum(before * hot, axis=0, keepdims=True).astype(jnp.int32)
    slot = slots_of(route, rank, plane, column, size, cap)
    data = [split(rows_ref[...]), split(cots_ref[...])]
    block = size * cap
    for part, step in enumerate(steps):
        pick = (
            lax.broadcasted_iota(jnp.int32, (block, count), 0) + step * block == slot
        ).astype(F32).astype(BF16)
        for kind, (high, low) in enumerate(data):
            rows = dot(pick, high, NN) + dot(pick, low, NN)
            for mask in range(size):
                outs[part * size + mask][kind] = rows[mask * cap : (mask + 1) * cap]


def pack(route_row, rows, cots, size, cap, groups, steps):
    count, width = rows.shape
    made = pl.pallas_call(
        functools.partial(pack_body, size, cap, groups, steps),
        out_shape=[jax.ShapeDtypeStruct((2, cap, width), F32)] * (len(steps) * size),
        compiler_params=pltpu.CompilerParams(vmem_limit_bytes=48 * 2**20),
        cost_estimate=pl.CostEstimate(
            flops=8 * count * count * width, bytes_accessed=12 * count * width, transcendentals=0
        ),
        name="pack",
    )(route_row, rows, cots)
    return [made[i * size : (i + 1) * size] for i in range(len(steps))]


def unpack_body(size, cap, groups, route_ref, *refs):
    out_ref = refs[-1]
    count = out_ref.shape[0]
    plane, column = position(size)
    route = route_ref[...]
    hot = (lax.broadcasted_iota(jnp.int32, (count, groups), 1) == route).astype(F32)
    ahead = (
        lax.broadcasted_iota(jnp.int32, (count, count), 1)
        < lax.broadcasted_iota(jnp.int32, (count, count), 0)
    ).astype(F32).astype(BF16)
    before = dot(ahead, hot.astype(BF16), NN)
    rank = jnp.sum(before * hot, axis=1, keepdims=True).astype(jnp.int32)
    slot = slots_of(route, rank, plane, column, size, cap)
    total = None
    for index, step in enumerate(sum(PAIRS, ())):
        pair, which = divmod(index, 2)
        rows = jnp.concatenate([refs[pair * size + m][which] for m in range(size)], axis=0)
        high, low = split(rows)
        at = lax.broadcasted_iota(jnp.int32, (count, size * cap), 1) + step * size * cap
        pick = (at == slot).astype(F32).astype(BF16)
        term = dot(pick, high, NN) + dot(pick, low, NN)
        total = term if total is None else total + term
    out_ref[...] = total


def unpack(route_col, pieces, size, cap, groups):
    count = route_col.shape[0]
    width = pieces[0].shape[-1]
    return pl.pallas_call(
        functools.partial(unpack_body, size, cap, groups),
        out_shape=jax.ShapeDtypeStruct((count, width), F32),
        compiler_params=pltpu.CompilerParams(vmem_limit_bytes=48 * 2**20),
        cost_estimate=pl.CostEstimate(
            flops=8 * count * count * width, bytes_accessed=12 * count * width, transcendentals=0
        ),
        name="unpack",
    )(route_col, *pieces)


def step_body(size, cap, layers, chunks, aliased, *refs):
    sent = refs[:size]
    mine, other = refs[size : size + 2]
    at = size + 2 + (size if aliased else 0)
    outs = refs[at : at + size]
    at += size
    keeps = refs[at : at + len(chunks)]
    sends = refs[at + len(chunks) : at + 2 * len(chunks)]
    at += 2 * len(chunks)
    wh, wl, ah, al, slope, full = refs[at:]
    width = full.shape[0]
    shard = mine.shape[1]
    core = lax.axis_index("replica")
    here = pl.multiple_of(core * shard, shard)
    there = pl.multiple_of(width - shard - core * shard, shard)

    for m in range(size):
        high, low = split(sent[m][0])
        ah[0, m * cap : (m + 1) * cap] = high
        al[0, m * cap : (m + 1) * cap] = low

    def weights(layer):
        high, low = split(mine[layer])
        wh[layer, pl.ds(here, shard)] = high
        wl[layer, pl.ds(here, shard)] = low
        high, low = split(other[layer])
        wh[layer, pl.ds(there, shard)] = high
        wl[layer, pl.ds(there, shard)] = low

    def forward(layer, _):
        weights(layer)
        pre = dot3(ah[layer], al[layer], wh[layer], wl[layer], NN)
        sigma = jax.nn.sigmoid(pre)
        high, low = split(pre * sigma)
        ah[layer + 1] = high
        al[layer + 1] = low
        slope[layer] = sigma * (1.0 + pre * (1.0 - sigma))
        return 0

    lax.fori_loop(0, layers - 1, forward, 0)
    last = layers - 1
    weights(last)
    result = dot3(ah[last], al[last], wh[last], wl[last], NN)
    for m in range(size):
        outs[m][0] = result[m * cap : (m + 1) * cap]

    delta = jnp.concatenate([sent[m][1] for m in range(size)], axis=0)
    dh, dl = split(delta)
    for keep, send, chunk in zip(keeps, sends, chunks):
        for layer in chunk:
            place = layer - min(chunk)
            full[...] = dot3(ah[layer], al[layer], dh, dl, TN)
            keep[place] = full[pl.ds(here, shard)]
            send[place] = full[pl.ds(there, shard)]
            if layer > 0:
                back = dot3(dh, dl, wh[layer], wl[layer], NT)
                dh, dl = split(back * slope[layer - 1])


def step_call(sent, mine, other, buffers, which, chunks):
    size = len(sent)
    cap, width = sent[0].shape[1:]
    layers, shard = mine.shape[:2]
    items = size * cap
    row_spec = pl.BlockSpec((2, cap, width), lambda i: (0, 0, 0))
    weight_spec = pl.BlockSpec((layers, shard, width), lambda i: (0, 0, 0))
    outs = [jax.ShapeDtypeStruct((2, cap, width), F32)] * size
    out_specs = [pl.BlockSpec((1, cap, width), lambda i: (which, 0, 0))] * size
    grads = [jax.ShapeDtypeStruct((len(c), shard, width), F32) for c in chunks] * 2
    grad_specs = [pl.BlockSpec((len(c), shard, width), lambda i: (0, 0, 0)) for c in chunks] * 2
    aliased = buffers is not None
    result = pl.pallas_call(
        functools.partial(step_body, size, cap, layers, chunks, aliased),
        grid=(1,),
        in_specs=[row_spec] * size
        + [weight_spec] * 2
        + [pl.BlockSpec(memory_space=pl.ANY)] * (size if aliased else 0),
        out_specs=out_specs + grad_specs,
        out_shape=outs + grads,
        input_output_aliases={size + 2 + m: m for m in range(size)} if aliased else {},
        scratch_shapes=[
            pltpu.VMEM((layers, width, width), BF16),
            pltpu.VMEM((layers, width, width), BF16),
            pltpu.VMEM((layers, items, width), BF16),
            pltpu.VMEM((layers, items, width), BF16),
            pltpu.VMEM((layers - 1, items, width), F32),
            pltpu.VMEM((width, width), F32),
        ],
        compiler_params=pltpu.CompilerParams(vmem_limit_bytes=48 * 2**20),
        cost_estimate=pl.CostEstimate(
            flops=18 * layers * items * width * width,
            bytes_accessed=4 * (3 * items * width + 2 * layers * width * width),
            transcendentals=layers * items * width,
        ),
        name="step",
    )(*sent, mine, other, *(buffers or ()))
    n = len(chunks)
    return result[:size], result[size : size + n], result[size + n :]


PAIRS = ((1, 2), (0, 3))


def chunks_of(layers, parts):
    order = list(range(layers - 1, -1, -1))
    parts = min(parts, layers)
    sizes = [layers // parts + (1 if i < layers % parts else 0) for i in range(parts)]
    cut, at = [], 0
    for n in sizes:
        cut.append(order[at : at + n])
        at += n
    return cut


PARTS = {0: 1, 1: 1, 2: 2, 3: 4}


def on_device(samples, routes, cotangent, weights, moment_one, moment_two):
    count = samples.shape[0]
    groups = lax.axis_size("expert")
    cap = 2 * count // groups
    size = groups // PLANES
    layers = weights.shape[0]
    route_row = routes.reshape(1, count)

    def plane_pairs(pairs):
        return [(a * size + p, b * size + p) for a, b in pairs for p in range(size)]

    def along(value, pairs):
        return lax.ppermute(value, "expert", plane_pairs(pairs))

    def swap_core(value):
        return lax.ppermute(value, "replica", [(0, 1), (1, 0)])

    def exchange(values):
        moved = [values[0]]
        for mask in range(1, size):
            moved.append(
                lax.ppermute(values[mask], "expert", [(e, e ^ mask) for e in range(groups)])
            )
        return moved

    SIDES = [(0, 1), (1, 0), (2, 3), (3, 2)]
    MIDDLE = [(1, 2), (2, 1)]
    OUTWARD = [(1, 0), (2, 3)]
    INWARD = [(0, 1), (3, 2)]

    own = weights[:, 0]
    side = along(own, SIDES)
    middle = along(own, MIDDLE)
    own_other = swap_core(own)
    arrived = {}
    for steps in PAIRS:
        packed = pack(route_row, samples, cotangent, size, cap, groups, steps)
        for step, values in zip(steps, packed):
            arrived[step] = exchange(values)
    side_in = along(side, MIDDLE)
    middle_out = along(middle, OUTWARD)
    side_out = along(side_in, OUTWARD)
    second = middle + middle_out
    third = side_in + side_out
    mats = [
        (own, own_other),
        (side, swap_core(side)),
        (second, swap_core(second)),
        (third, swap_core(third)),
    ]
    outputs = {}
    sums = {}
    for i, steps in enumerate(PAIRS):
        buffers = None
        for which, step in enumerate(steps):
            buffers, keeps, sends = step_call(
                arrived[step], *mats[step], buffers, which, chunks_of(layers, PARTS[step])
            )
            sums[step] = [keep + swap_core(send) for keep, send in zip(keeps, sends)]
        outputs[i] = exchange(buffers)

    zero, one = sums[0][0], sums[1][0]
    first_in = along(one, INWARD)
    second_mid = [along(value + along(value, INWARD), MIDDLE) for value in sums[2]]
    third_out = []
    cut = chunks_of(layers, PARTS[3])
    held = lax.optimization_barrier([one[min(c) : max(c) + 1] for c in cut])
    for j, value in enumerate(sums[3]):
        inward = value + along(value, INWARD)
        passed = held[j] + along(inward, MIDDLE)
        third_out.append(along(passed, OUTWARD))
    grad = (
        zero
        + first_in
        + jnp.concatenate(second_mid[::-1], axis=0)
        + jnp.concatenate(third_out[::-1], axis=0)
    )[:, None]
    new_one = 0.9 * moment_one + 0.1 * grad
    new_two = 0.999 * moment_two + 0.001 * grad * grad
    new_w = weights - 0.01 * (new_one / CORR_ONE) / (jnp.sqrt(new_two / CORR_TWO) + 1e-08)
    result = unpack(routes, outputs[0] + outputs[1], size, cap, groups)
    return (result, new_w, new_one, new_two)


def solution(mesh):
    placed = (
        P(("expert", "replica"), None),
        P(("expert", "replica"), None),
        P(("expert", "replica"), None),
        P(None, "expert", "replica", None),
        P(None, "expert", "replica", None),
        P(None, "expert", "replica", None),
    )
    return jax.shard_map(
        on_device,
        mesh=mesh,
        in_specs=placed,
        out_specs=(
            P(("expert", "replica"), None),
            P(None, "expert", "replica", None),
            P(None, "expert", "replica", None),
            P(None, "expert", "replica", None),
        ),
        check_vma=False,
    )
```

```python
import functools

import jax
import jax.numpy as jnp
from jax import lax
from jax.experimental import pallas as pl
from jax.experimental.pallas import tpu as pltpu
from jax.sharding import PartitionSpec as P


CORR_ONE = 0.9999734386011124
CORR_TWO = 0.09520785288629038
PLANES = 4

F32 = jnp.float32
BF16 = jnp.bfloat16


def split(value):
    high = value.astype(BF16)
    return high, (value - high.astype(F32)).astype(BF16)


def dot(a, b, dims):
    return lax.dot_general(a, b, (dims, ((), ())), preferred_element_type=F32)


def dot3(ah, al, bh, bl, dims):
    return dot(ah, bh, dims) + (dot(ah, bl, dims) + dot(al, bh, dims))


NN = ((1,), (0,))
NT = ((1,), (1,))
TN = ((0,), (0,))


def slots_of(route, rank, plane, column, size, cap):
    own = jnp.right_shift(route, size.bit_length() - 1)
    chip = jnp.bitwise_and(route, size - 1)
    near = jnp.bitwise_xor(own, plane)
    inner = jnp.bitwise_and(jnp.bitwise_xor(jnp.right_shift(own, 1), own), 1)
    step = jnp.where(near < 2, near, 3 - inner)
    mask = jnp.bitwise_xor(chip, column)
    return (step * size + mask) * cap + rank


def position(size):
    at = lax.axis_index("expert")
    return jnp.right_shift(at, size.bit_length() - 1), jnp.bitwise_and(at, size - 1)


def slot_column(size, cap, groups, route):
    count = route.shape[0]
    plane, column = position(size)
    hot = (lax.broadcasted_iota(jnp.int32, (count, groups), 1) == route).astype(F32)
    ahead = (
        lax.broadcasted_iota(jnp.int32, (count, count), 1)
        < lax.broadcasted_iota(jnp.int32, (count, count), 0)
    ).astype(F32).astype(BF16)
    before = dot(ahead, hot.astype(BF16), NN)
    rank = jnp.sum(before * hot, axis=1, keepdims=True).astype(jnp.int32)
    return slots_of(route, rank, plane, column, size, cap)


def pack_body(size, cap, groups, steps, with_column, *refs):
    route_ref, rows_ref, cots_ref = refs[:3]
    outs = refs[3:]
    if with_column:
        outs[-1][...] = slot_column(size, cap, groups, outs[0][...])
        outs = outs[1:-1]
    count, _ = rows_ref.shape
    plane, column = position(size)
    route = route_ref[...]
    hot = (lax.broadcasted_iota(jnp.int32, (groups, count), 0) == route).astype(F32)
    ahead = (
        lax.broadcasted_iota(jnp.int32, (count, count), 0)
        < lax.broadcasted_iota(jnp.int32, (count, count), 1)
    ).astype(F32).astype(BF16)
    before = dot(hot.astype(BF16), ahead, NN)
    rank = jnp.sum(before * hot, axis=0, keepdims=True).astype(jnp.int32)
    slot = slots_of(route, rank, plane, column, size, cap)
    data = [split(rows_ref[...]), split(cots_ref[...])]
    block = size * cap
    for part, step in enumerate(steps):
        pick = (
            lax.broadcasted_iota(jnp.int32, (block, count), 0) + step * block == slot
        ).astype(F32).astype(BF16)
        for kind, (high, low) in enumerate(data):
            rows = dot(pick, high, NN) + dot(pick, low, NN)
            for mask in range(size):
                outs[part * size + mask][kind] = rows[mask * cap : (mask + 1) * cap]


def pack(route_row, rows, cots, size, cap, groups, steps, route_col=None):
    count, width = rows.shape
    with_column = route_col is not None
    column = [pltpu.HBM((count, 1), jnp.int32)] if with_column else []
    rows, cots = (pltpu.with_memory_space_constraint(v, pltpu.HBM) for v in (rows, cots))
    row_spec = pl.BlockSpec((count, width), lambda i: (0, 0))
    out_spec = pl.BlockSpec((2, cap, width), lambda i: (0, 0, 0))
    in_specs = [pl.BlockSpec((1, count), lambda i: (0, 0)), row_spec, row_spec]
    col_spec = pl.BlockSpec((count, 1), lambda i: (0, 0))
    made = pl.pallas_call(
        functools.partial(pack_body, size, cap, groups, steps, with_column),
        grid=(1,),
        in_specs=in_specs + [col_spec] * with_column,
        out_specs=[out_spec] * (len(steps) * size) + [col_spec] * with_column,
        out_shape=[
            (pltpu.HBM if m == 0 else jax.ShapeDtypeStruct)((2, cap, width), F32)
            for m in list(range(size)) * len(steps)
        ]
        + column,
        compiler_params=pltpu.CompilerParams(vmem_limit_bytes=48 * 2**20),
        cost_estimate=pl.CostEstimate(
            flops=8 * count * count * width, bytes_accessed=12 * count * width, transcendentals=0
        ),
        name="pack",
    )(route_row, rows, cots, *([route_col] if with_column else []))
    return [made[i * size : (i + 1) * size] for i in range(len(steps))], made[-1]


def unpack_body(size, cap, steps, added, slot_ref, *refs):
    out_ref = refs[-1]
    count = out_ref.shape[0]
    slot = slot_ref[...]
    total = refs[size][...] if added else None
    for which, step in enumerate(steps):
        rows = jnp.concatenate([refs[m][which] for m in range(size)], axis=0)
        high, low = split(rows)
        at = lax.broadcasted_iota(jnp.int32, (count, size * cap), 1) + step * size * cap
        pick = (at == slot).astype(F32).astype(BF16)
        term = dot(pick, high, NN) + dot(pick, low, NN)
        total = term if total is None else total + term
    out_ref[...] = total


def unpack(slot_col, pieces, before, steps, cap):
    size = len(pieces)
    count = slot_col.shape[0]
    width = pieces[0].shape[-1]
    added = before is not None
    return pl.pallas_call(
        functools.partial(unpack_body, size, cap, steps, added),
        out_shape=jax.ShapeDtypeStruct((count, width), F32),
        compiler_params=pltpu.CompilerParams(vmem_limit_bytes=48 * 2**20),
        cost_estimate=pl.CostEstimate(
            flops=4 * count * count * width, bytes_accessed=12 * count * width, transcendentals=0
        ),
        name="unpack",
    )(slot_col, *pieces, *([before] if added else []))


def adam_body(w_ref, one_ref, two_ref, base_ref, mid_ref, far_ref, *refs):
    new_w, new_one, new_two = refs[-3:]
    grad = base_ref[0] + (mid_ref[0] + far_ref[0])
    one = 0.9 * one_ref[0, 0] + 0.1 * grad
    two = 0.999 * two_ref[0, 0] + 0.001 * grad * grad
    new_one[0, 0] = one
    new_two[0, 0] = two
    new_w[0, 0] = w_ref[0, 0] - 0.01 * (one / CORR_ONE) / (jnp.sqrt(two / CORR_TWO) + 1e-08)


def adam(weights, moment_one, moment_two, base, mid, far, chunk, mid_low, buffers):
    _, _, shard, width = weights.shape
    low = min(chunk)
    whole = pl.BlockSpec((1, 1, shard, width), lambda i: (low + i, 0, 0, 0))
    aliased = buffers is not None
    return pl.pallas_call(
        adam_body,
        grid=(len(chunk),),
        in_specs=[whole] * 3
        + [
            pl.BlockSpec((1, shard, width), lambda i: (low + i, 0, 0)),
            pl.BlockSpec((1, shard, width), lambda i: (low - mid_low + i, 0, 0)),
            pl.BlockSpec((1, shard, width), lambda i: (i, 0, 0)),
        ]
        + [pl.BlockSpec(memory_space=pl.ANY)] * (3 if aliased else 0),
        out_specs=[whole] * 3,
        out_shape=[jax.ShapeDtypeStruct(weights.shape, F32)] * 3,
        input_output_aliases={6 + i: i for i in range(3)} if aliased else {},
        compiler_params=pltpu.CompilerParams(vmem_limit_bytes=48 * 2**20),
        cost_estimate=pl.CostEstimate(
            flops=20 * len(chunk) * shard * width,
            bytes_accessed=36 * len(chunk) * shard * width,
            transcendentals=len(chunk) * shard * width,
        ),
        name="adam",
    )(weights, moment_one, moment_two, base, mid, far, *(buffers or ()))


def step_body(size, cap, layers, chunks, aliased, *refs):
    sent = refs[:size]
    mine, other = refs[size : size + 2]
    at = size + 2 + (size if aliased else 0)
    outs = refs[at : at + size]
    at += size
    keeps = refs[at : at + len(chunks)]
    sends = refs[at + len(chunks) : at + 2 * len(chunks)]
    at += 2 * len(chunks)
    wh, wl, ah, al, slope, full = refs[at:]
    width = full.shape[0]
    shard = mine.shape[1]
    core = lax.axis_index("replica")
    here = pl.multiple_of(core * shard, shard)
    there = pl.multiple_of(width - shard - core * shard, shard)

    for m in range(size):
        high, low = split(sent[m][0])
        ah[0, m * cap : (m + 1) * cap] = high
        al[0, m * cap : (m + 1) * cap] = low

    def weights(layer):
        high, low = split(mine[layer])
        wh[layer, pl.ds(here, shard)] = high
        wl[layer, pl.ds(here, shard)] = low
        high, low = split(other[layer])
        wh[layer, pl.ds(there, shard)] = high
        wl[layer, pl.ds(there, shard)] = low

    def forward(layer, _):
        weights(layer)
        pre = dot3(ah[layer], al[layer], wh[layer], wl[layer], NN)
        sigma = jax.nn.sigmoid(pre)
        high, low = split(pre * sigma)
        ah[layer + 1] = high
        al[layer + 1] = low
        slope[layer] = sigma * (1.0 + pre * (1.0 - sigma))
        return 0

    lax.fori_loop(0, layers - 1, forward, 0)
    last = layers - 1
    weights(last)
    result = dot3(ah[last], al[last], wh[last], wl[last], NN)
    for m in range(size):
        outs[m][0] = result[m * cap : (m + 1) * cap]

    delta = jnp.concatenate([sent[m][1] for m in range(size)], axis=0)
    dh, dl = split(delta)
    for keep, send, chunk in zip(keeps, sends, chunks):
        for layer in chunk:
            place = layer - min(chunk)
            full[...] = dot3(ah[layer], al[layer], dh, dl, TN)
            keep[place] = full[pl.ds(here, shard)]
            send[place] = full[pl.ds(there, shard)]
            if layer > 0:
                back = dot3(dh, dl, wh[layer], wl[layer], NT)
                dh, dl = split(back * slope[layer - 1])


def step_call(sent, mine, other, buffers, which, chunks):
    size = len(sent)
    cap, width = sent[0].shape[1:]
    layers, shard = mine.shape[:2]
    items = size * cap
    row_spec = pl.BlockSpec((2, cap, width), lambda i: (0, 0, 0))
    weight_spec = pl.BlockSpec((layers, shard, width), lambda i: (0, 0, 0))
    outs = [pltpu.HBM((2, cap, width), F32)] * size
    out_specs = [pl.BlockSpec((1, cap, width), lambda i: (which, 0, 0))] * size
    grads = [jax.ShapeDtypeStruct((len(c), shard, width), F32) for c in chunks] * 2
    grad_specs = [pl.BlockSpec((len(c), shard, width), lambda i: (0, 0, 0)) for c in chunks] * 2
    aliased = buffers is not None
    result = pl.pallas_call(
        functools.partial(step_body, size, cap, layers, chunks, aliased),
        grid=(1,),
        in_specs=[row_spec] * size
        + [weight_spec] * 2
        + [pl.BlockSpec(memory_space=pl.ANY)] * (size if aliased else 0),
        out_specs=out_specs + grad_specs,
        out_shape=outs + grads,
        input_output_aliases={size + 2 + m: m for m in range(size)} if aliased else {},
        scratch_shapes=[
            pltpu.VMEM((layers, width, width), BF16),
            pltpu.VMEM((layers, width, width), BF16),
            pltpu.VMEM((layers, items, width), BF16),
            pltpu.VMEM((layers, items, width), BF16),
            pltpu.VMEM((layers - 1, items, width), F32),
            pltpu.VMEM((width, width), F32),
        ],
        compiler_params=pltpu.CompilerParams(vmem_limit_bytes=48 * 2**20),
        cost_estimate=pl.CostEstimate(
            flops=18 * layers * items * width * width,
            bytes_accessed=4 * (3 * items * width + 2 * layers * width * width),
            transcendentals=layers * items * width,
        ),
        name="step",
    )(*sent, mine, other, *(buffers or ()))
    n = len(chunks)
    return result[:size], result[size : size + n], result[size + n :]


PAIRS = ((1, 2), (0, 3))


def chunks_of(layers, step):
    order = list(range(layers - 1, -1, -1))
    first, second = layers - layers // 3 * 2, layers // 3
    cut = [order[:first], order[first : first + second], order[first + second :]]
    return cut if step > 1 else [order]


def on_device(samples, routes, cotangent, weights, moment_one, moment_two):
    count = samples.shape[0]
    groups = lax.axis_size("expert")
    cap = 2 * count // groups
    size = groups // PLANES
    layers = weights.shape[0]
    route_row = routes.reshape(1, count)

    def plane_pairs(pairs):
        return [(a * size + p, b * size + p) for a, b in pairs for p in range(size)]

    def along(value, pairs):
        return lax.ppermute(value, "expert", plane_pairs(pairs))

    def swap_core(value):
        return lax.ppermute(value, "replica", [(0, 1), (1, 0)])

    def exchange(values):
        moved = [values[0]]
        for mask in range(1, size):
            moved.append(
                lax.ppermute(values[mask], "expert", [(e, e ^ mask) for e in range(groups)])
            )
        return moved

    SIDES = [(0, 1), (1, 0), (2, 3), (3, 2)]
    MIDDLE = [(1, 2), (2, 1)]
    OUTWARD = [(1, 0), (2, 3)]
    INWARD = [(0, 1), (3, 2)]
    FAR = [(1, 3), (2, 0)]
    plane, _ = position(size)
    inner = jnp.logical_and(plane > 0, plane < PLANES - 1)

    own = weights[:, 0]
    side = along(own, SIDES)
    middle = along(own, MIDDLE)
    own_other = swap_core(own)
    arrived = {}
    for i, steps in enumerate(PAIRS):
        packed, slot_col = pack(
            route_row, samples, cotangent, size, cap, groups, steps, routes if i else None
        )
        for step, values in zip(steps, packed):
            arrived[step] = exchange(values)
    side_in = along(side, MIDDLE)
    middle_out = along(middle, OUTWARD)
    second = middle + middle_out

    mats = {
        0: lambda: (own, own_other),
        1: lambda: (side, swap_core(side)),
        2: lambda: (second, swap_core(second)),
        3: lambda: (third, swap_core(third)),
    }
    outputs = {}
    sums = {}
    for i, steps in enumerate(PAIRS):
        buffers = None
        for which, step in enumerate(steps):
            if step == 3:
                late, _ = lax.optimization_barrier((p3, buffers[0]))
                third = jnp.where(inner, side_in, late)
            pair = mats[step]()
            buffers, keeps, sends = step_call(
                arrived[step], *pair, buffers, which, chunks_of(layers, step)
            )
            sums[step] = [keep + swap_core(send) for keep, send in zip(keeps, sends)]
            if step == 1:
                one = sums[1][0]
                p3 = along(jnp.where(inner, side_in, one), SIDES)
        outputs[i] = exchange(buffers)

    zero = sums[0][0]
    cut_two, cut_three = chunks_of(layers, 2), chunks_of(layers, 3)
    p4, mid = [], []
    for value, c in zip(sums[2], cut_two):
        back = along(jnp.where(inner, one[min(c) : max(c) + 1], value), SIDES)
        p4.append(back)
        mid.append(along(value + back, MIDDLE))
    kept, sides, *late = lax.optimization_barrier((zero, p3, *p4))
    base = kept + jnp.where(inner, sides, jnp.concatenate(late[::-1], axis=0))
    updated = None
    for value, c in zip(sums[3], cut_three):
        passed = value + along(value, INWARD)
        far = along(passed, FAR)
        k = next(k for k, d in enumerate(cut_two) if min(c) in d)
        updated = adam(
            weights, moment_one, moment_two, base, mid[k], far, c, min(cut_two[k]), updated
        )
    result = None
    for i, steps in enumerate(PAIRS):
        result = unpack(slot_col, outputs[i], result, steps, cap)
    return (result, *updated)


def solution(mesh):
    placed = (
        P(("expert", "replica"), None),
        P(("expert", "replica"), None),
        P(("expert", "replica"), None),
        P(None, "expert", "replica", None),
        P(None, "expert", "replica", None),
        P(None, "expert", "replica", None),
    )
    return jax.shard_map(
        on_device,
        mesh=mesh,
        in_specs=placed,
        out_specs=(
            P(("expert", "replica"), None),
            P(None, "expert", "replica", None),
            P(None, "expert", "replica", None),
            P(None, "expert", "replica", None),
        ),
        check_vma=False,
    )
```

```python
import functools

import jax
import jax.numpy as jnp
from jax import lax
from jax.experimental import pallas as pl
from jax.experimental.pallas import tpu as pltpu
from jax.sharding import PartitionSpec as P


CORR_ONE = 0.9999734386011124
CORR_TWO = 0.09520785288629038
PLANES = 4

F32 = jnp.float32
BF16 = jnp.bfloat16


def split(value):
    high = value.astype(BF16)
    return high, (value - high.astype(F32)).astype(BF16)


def dot(a, b, dims):
    return lax.dot_general(a, b, (dims, ((), ())), preferred_element_type=F32)


def dot3(ah, al, bh, bl, dims):
    return dot(ah, bh, dims) + (dot(ah, bl, dims) + dot(al, bh, dims))


NN = ((1,), (0,))
NT = ((1,), (1,))
TN = ((0,), (0,))


def slots_of(route, rank, plane, column, size, cap):
    own = jnp.right_shift(route, size.bit_length() - 1)
    chip = jnp.bitwise_and(route, size - 1)
    near = jnp.bitwise_xor(own, plane)
    inner = jnp.bitwise_and(jnp.bitwise_xor(jnp.right_shift(own, 1), own), 1)
    step = jnp.where(near < 2, near, 3 - inner)
    mask = jnp.bitwise_xor(chip, column)
    return (step * size + mask) * cap + rank


def position(size):
    at = lax.axis_index("expert")
    return jnp.right_shift(at, size.bit_length() - 1), jnp.bitwise_and(at, size - 1)


def slot_column(size, cap, groups, route):
    count = route.shape[0]
    plane, column = position(size)
    hot = (lax.broadcasted_iota(jnp.int32, (count, groups), 1) == route).astype(F32)
    ahead = (
        lax.broadcasted_iota(jnp.int32, (count, count), 1)
        < lax.broadcasted_iota(jnp.int32, (count, count), 0)
    ).astype(F32).astype(BF16)
    before = dot(ahead, hot.astype(BF16), NN)
    rank = jnp.sum(before * hot, axis=1, keepdims=True).astype(jnp.int32)
    return slots_of(route, rank, plane, column, size, cap)


def pack_body(size, cap, groups, steps, with_column, *refs):
    route_ref, rows_ref, cots_ref = refs[:3]
    outs = refs[3:]
    if with_column:
        outs[-1][...] = slot_column(size, cap, groups, outs[0][...])
        outs = outs[1:-1]
    count, _ = rows_ref.shape
    plane, column = position(size)
    route = route_ref[...]
    hot = (lax.broadcasted_iota(jnp.int32, (groups, count), 0) == route).astype(F32)
    ahead = (
        lax.broadcasted_iota(jnp.int32, (count, count), 0)
        < lax.broadcasted_iota(jnp.int32, (count, count), 1)
    ).astype(F32).astype(BF16)
    before = dot(hot.astype(BF16), ahead, NN)
    rank = jnp.sum(before * hot, axis=0, keepdims=True).astype(jnp.int32)
    slot = slots_of(route, rank, plane, column, size, cap)
    data = [split(rows_ref[...]), split(cots_ref[...])]
    block = size * cap
    for part, step in enumerate(steps):
        pick = (
            lax.broadcasted_iota(jnp.int32, (block, count), 0) + step * block == slot
        ).astype(F32).astype(BF16)
        for kind, (high, low) in enumerate(data):
            rows = dot(pick, high, NN) + dot(pick, low, NN)
            for mask in range(size):
                outs[part * size + mask][kind] = rows[mask * cap : (mask + 1) * cap]


def pack(route_row, rows, cots, size, cap, groups, steps, route_col=None):
    count, width = rows.shape
    with_column = route_col is not None
    column = [pltpu.HBM((count, 1), jnp.int32)] if with_column else []
    rows, cots = (pltpu.with_memory_space_constraint(v, pltpu.HBM) for v in (rows, cots))
    row_spec = pl.BlockSpec((count, width), lambda i: (0, 0))
    out_spec = pl.BlockSpec((2, cap, width), lambda i: (0, 0, 0))
    in_specs = [pl.BlockSpec((1, count), lambda i: (0, 0)), row_spec, row_spec]
    col_spec = pl.BlockSpec((count, 1), lambda i: (0, 0))
    made = pl.pallas_call(
        functools.partial(pack_body, size, cap, groups, steps, with_column),
        grid=(1,),
        in_specs=in_specs + [col_spec] * with_column,
        out_specs=[out_spec] * (len(steps) * size) + [col_spec] * with_column,
        out_shape=[
            (pltpu.HBM if m == 0 else jax.ShapeDtypeStruct)((2, cap, width), F32)
            for m in list(range(size)) * len(steps)
        ]
        + column,
        compiler_params=pltpu.CompilerParams(vmem_limit_bytes=48 * 2**20),
        cost_estimate=pl.CostEstimate(
            flops=8 * count * count * width, bytes_accessed=12 * count * width, transcendentals=0
        ),
        name="pack",
    )(route_row, rows, cots, *([route_col] if with_column else []))
    return [made[i * size : (i + 1) * size] for i in range(len(steps))], made[-1]


def unpack_body(size, cap, steps, added, slot_ref, *refs):
    out_ref = refs[-1]
    count = out_ref.shape[0]
    slot = slot_ref[...]
    total = refs[size][...] if added else None
    for which, step in enumerate(steps):
        rows = jnp.concatenate([refs[m][which] for m in range(size)], axis=0)
        high, low = split(rows)
        at = lax.broadcasted_iota(jnp.int32, (count, size * cap), 1) + step * size * cap
        pick = (at == slot).astype(F32).astype(BF16)
        term = dot(pick, high, NN) + dot(pick, low, NN)
        total = term if total is None else total + term
    out_ref[...] = total


def unpack(slot_col, pieces, before, steps, cap):
    size = len(pieces)
    count = slot_col.shape[0]
    width = pieces[0].shape[-1]
    added = before is not None
    return pl.pallas_call(
        functools.partial(unpack_body, size, cap, steps, added),
        out_shape=jax.ShapeDtypeStruct((count, width), F32),
        compiler_params=pltpu.CompilerParams(vmem_limit_bytes=48 * 2**20),
        cost_estimate=pl.CostEstimate(
            flops=4 * count * count * width, bytes_accessed=12 * count * width, transcendentals=0
        ),
        name="unpack",
    )(slot_col, *pieces, *([before] if added else []))


def adam_body(w_ref, one_ref, two_ref, base_ref, far_ref, last_ref, *refs):
    new_w, new_one, new_two = refs[-3:]
    grad = base_ref[0] + (far_ref[0] + last_ref[0])
    one = 0.9 * one_ref[0, 0] + 0.1 * grad
    two = 0.999 * two_ref[0, 0] + 0.001 * grad * grad
    new_one[0, 0] = one
    new_two[0, 0] = two
    new_w[0, 0] = w_ref[0, 0] - 0.01 * (one / CORR_ONE) / (jnp.sqrt(two / CORR_TWO) + 1e-08)


def adam(weights, moment_one, moment_two, base, far, last, chunk, buffers):
    _, _, shard, width = weights.shape
    low = min(chunk)
    whole = pl.BlockSpec((1, 1, shard, width), lambda i: (low + i, 0, 0, 0))
    aliased = buffers is not None
    return pl.pallas_call(
        adam_body,
        grid=(len(chunk),),
        in_specs=[whole] * 3
        + [pl.BlockSpec((1, shard, width), lambda i: (low + i, 0, 0))] * 2
        + [
            pl.BlockSpec((1, shard, width), lambda i: (i, 0, 0)),
        ]
        + [pl.BlockSpec(memory_space=pl.ANY)] * (3 if aliased else 0),
        out_specs=[whole] * 3,
        out_shape=[jax.ShapeDtypeStruct(weights.shape, F32)] * 3,
        input_output_aliases={6 + i: i for i in range(3)} if aliased else {},
        compiler_params=pltpu.CompilerParams(vmem_limit_bytes=48 * 2**20),
        cost_estimate=pl.CostEstimate(
            flops=20 * len(chunk) * shard * width,
            bytes_accessed=32 * len(chunk) * shard * width,
            transcendentals=len(chunk) * shard * width,
        ),
        name="adam",
    )(weights, moment_one, moment_two, base, far, last, *(buffers or ()))


def step_body(size, cap, layers, chunks, aliased, forwarded, *refs):
    sent = refs[:size]
    mine, other = refs[size : size + 2]
    at = size + 2
    passed = refs[at] if forwarded else None
    at += int(forwarded) + (size if aliased else 0)
    outs = refs[at : at + size]
    at += size
    back_out = refs[at] if forwarded else None
    at += int(forwarded)
    items = size * cap
    keeps = refs[at : at + len(chunks)]
    sends = refs[at + len(chunks) : at + 2 * len(chunks)]
    at += 2 * len(chunks)
    wh, wl, ah, al, slope, full = refs[at:]
    width = full.shape[0]
    shard = mine.shape[1]
    core = lax.axis_index("replica")
    here = pl.multiple_of(core * shard, shard)
    there = pl.multiple_of(width - shard - core * shard, shard)

    for m in range(size):
        high, low = split(sent[m][0])
        ah[0, m * cap : (m + 1) * cap] = high
        al[0, m * cap : (m + 1) * cap] = low
        if forwarded:
            high, low = split(passed[m, 0])
            ah[0, items + m * cap : items + (m + 1) * cap] = high
            al[0, items + m * cap : items + (m + 1) * cap] = low

    def weights(layer):
        high, low = split(mine[layer])
        wh[layer, pl.ds(here, shard)] = high
        wl[layer, pl.ds(here, shard)] = low
        high, low = split(other[layer])
        wh[layer, pl.ds(there, shard)] = high
        wl[layer, pl.ds(there, shard)] = low

    def forward(layer, _):
        weights(layer)
        pre = dot3(ah[layer], al[layer], wh[layer], wl[layer], NN)
        sigma = jax.nn.sigmoid(pre)
        high, low = split(pre * sigma)
        ah[layer + 1] = high
        al[layer + 1] = low
        slope[layer] = sigma * (1.0 + pre * (1.0 - sigma))
        return 0

    lax.fori_loop(0, layers - 1, forward, 0)
    last = layers - 1
    weights(last)
    result = dot3(ah[last], al[last], wh[last], wl[last], NN)
    for m in range(size):
        outs[m][0] = result[m * cap : (m + 1) * cap]
        if forwarded:
            back_out[m] = result[items + m * cap : items + (m + 1) * cap]

    delta = [sent[m][1] for m in range(size)]
    if forwarded:
        delta += [passed[m, 1] for m in range(size)]
    dh, dl = split(jnp.concatenate(delta, axis=0))
    for keep, send, chunk in zip(keeps, sends, chunks):
        for layer in chunk:
            place = layer - min(chunk)
            full[...] = dot3(ah[layer], al[layer], dh, dl, TN)
            keep[place] = full[pl.ds(here, shard)]
            send[place] = full[pl.ds(there, shard)]
            if layer > 0:
                back = dot3(dh, dl, wh[layer], wl[layer], NT)
                dh, dl = split(back * slope[layer - 1])


def step_call(sent, mine, other, buffers, which, chunks, passed=None):
    size = len(sent)
    cap, width = sent[0].shape[1:]
    layers, shard = mine.shape[:2]
    forwarded = passed is not None
    aliased = buffers is not None
    items = size * cap * (2 if forwarded else 1)
    row_spec = pl.BlockSpec((2, cap, width), lambda i: (0, 0, 0))
    pass_spec = pl.BlockSpec((size, 2, cap, width), lambda i: (0, 0, 0, 0))
    back_spec = pl.BlockSpec((size, cap, width), lambda i: (0, 0, 0))
    weight_spec = pl.BlockSpec((layers, shard, width), lambda i: (0, 0, 0))
    outs = [pltpu.HBM((2, cap, width), F32)] * size
    out_specs = [pl.BlockSpec((1, cap, width), lambda i: (which, 0, 0))] * size
    back = [jax.ShapeDtypeStruct((size, cap, width), F32)] * forwarded
    grads = [jax.ShapeDtypeStruct((len(c), shard, width), F32) for c in chunks] * 2
    grad_specs = [pl.BlockSpec((len(c), shard, width), lambda i: (0, 0, 0)) for c in chunks] * 2
    first = size + 2 + int(forwarded)
    result = pl.pallas_call(
        functools.partial(step_body, size, cap, layers, chunks, aliased, forwarded),
        grid=(1,),
        in_specs=[row_spec] * size
        + [weight_spec] * 2
        + [pass_spec] * forwarded
        + [pl.BlockSpec(memory_space=pl.ANY)] * (size if aliased else 0),
        out_specs=out_specs + [back_spec] * forwarded + grad_specs,
        out_shape=outs + back + grads,
        input_output_aliases={first + m: m for m in range(size)} if aliased else {},
        scratch_shapes=[
            pltpu.VMEM((layers, width, width), BF16),
            pltpu.VMEM((layers, width, width), BF16),
            pltpu.VMEM((layers, items, width), BF16),
            pltpu.VMEM((layers, items, width), BF16),
            pltpu.VMEM((layers - 1, items, width), F32),
            pltpu.VMEM((width, width), F32),
        ],
        compiler_params=pltpu.CompilerParams(vmem_limit_bytes=48 * 2**20),
        cost_estimate=pl.CostEstimate(
            flops=18 * layers * items * width * width,
            bytes_accessed=4 * (3 * items * width + 2 * layers * width * width),
            transcendentals=layers * items * width,
        ),
        name="step",
    )(*sent, mine, other, *([passed] if forwarded else []), *(buffers or ()))
    n = len(chunks)
    at = size + int(forwarded)
    return result[:at], result[at : at + n], result[at + n :]


LEAVING = (3, 1, 0, 2)


def chunks_of(layers, step):
    order = list(range(layers - 1, -1, -1))
    first, second = layers - layers // 3 * 2, layers // 3
    cut = [order[:first], order[first : first + second], order[first + second :]]
    return cut if step == 2 else [order]


def on_device(samples, routes, cotangent, weights, moment_one, moment_two):
    count = samples.shape[0]
    groups = lax.axis_size("expert")
    cap = 2 * count // groups
    size = groups // PLANES
    layers = weights.shape[0]
    route_row = routes.reshape(1, count)

    def plane_pairs(pairs):
        return [(a * size + p, b * size + p) for a, b in pairs for p in range(size)]

    def along(value, pairs):
        return lax.ppermute(value, "expert", plane_pairs(pairs))

    def swap_core(value):
        return lax.ppermute(value, "replica", [(0, 1), (1, 0)])

    def exchange(values):
        moved = [values[0]]
        for mask in range(1, size):
            moved.append(
                lax.ppermute(values[mask], "expert", [(e, e ^ mask) for e in range(groups)])
            )
        return moved

    SIDES = [(0, 1), (1, 0), (2, 3), (3, 2)]
    MIDDLE = [(1, 2), (2, 1)]
    OUTWARD = [(1, 0), (2, 3)]
    INWARD = [(0, 1), (3, 2)]
    FAR = [(1, 3), (2, 0)]
    plane, _ = position(size)
    inner = jnp.logical_and(plane > 0, plane < PLANES - 1)

    own = weights[:, 0]
    side = along(own, SIDES)
    middle = along(own, MIDDLE)
    own_other = swap_core(own)
    arrived = {}
    packed, slot_col = pack(
        route_row, samples, cotangent, size, cap, groups, LEAVING, routes
    )
    for step, values in zip(LEAVING, packed):
        arrived[step] = exchange(values)
    beyond = along(side, MIDDLE)
    middle_out = along(middle, OUTWARD)
    passed = along(jnp.stack(arrived[3]), INWARD)
    second = middle + middle_out
    mats = {0: (own, own_other)}
    for step, value in ((1, side), (3, beyond), (2, second)):
        mats[step] = (value, swap_core(value))

    sums = {}

    def run(step, buffers, which, extra=None):
        outs, keeps, sends = step_call(
            arrived[step], *mats[step], buffers, which, chunks_of(layers, step), extra
        )
        sums[step] = []
        for keep, send in zip(keeps, sends):
            sums[step].append(keep + swap_core(send))
        return outs

    near = run(1, None, 0)
    rest = run(0, None, 0)
    *rest, back = run(3, rest, 1, passed)
    near = run(2, near, 1)
    back = along(back, OUTWARD)
    rest = [
        jnp.stack([value[0], jnp.where(inner, value[1], back[m])])
        for m, value in enumerate(rest)
    ]
    outputs = [exchange(near), exchange(rest)]

    zero, one, three = sums[0][0], sums[1][0], sums[3][0]
    from_side = along(one, SIDES)
    from_far = along(three, FAR)
    base = zero + from_side
    updated = None
    for value, c in zip(sums[2], chunks_of(layers, 2)):
        joined = value + along(value, INWARD)
        last = along(joined, MIDDLE)
        updated = adam(weights, moment_one, moment_two, base, from_far, last, c, updated)
    result = None
    for i, steps in enumerate(((1, 2), (0, 3))):
        result = unpack(slot_col, outputs[i], result, steps, cap)
    return (result, *updated)


def solution(mesh):
    placed = (
        P(("expert", "replica"), None),
        P(("expert", "replica"), None),
        P(("expert", "replica"), None),
        P(None, "expert", "replica", None),
        P(None, "expert", "replica", None),
        P(None, "expert", "replica", None),
    )
    return jax.shard_map(
        on_device,
        mesh=mesh,
        in_specs=placed,
        out_specs=(
            P(("expert", "replica"), None),
            P(None, "expert", "replica", None),
            P(None, "expert", "replica", None),
            P(None, "expert", "replica", None),
        ),
        check_vma=False,
    )
```

```python
import functools

import jax
import jax.numpy as jnp
from jax import lax
from jax.experimental import pallas as pl
from jax.experimental.pallas import tpu as pltpu
from jax.sharding import PartitionSpec as P


CORR_ONE = 0.9999734386011124
CORR_TWO = 0.09520785288629038
PLANES = 4

F32 = jnp.float32
BF16 = jnp.bfloat16


def split(value):
    high = value.astype(BF16)
    return high, (value - high.astype(F32)).astype(BF16)


def dot(a, b, dims):
    return lax.dot_general(a, b, (dims, ((), ())), preferred_element_type=F32)


def dot3(ah, al, bh, bl, dims):
    return dot(ah, bh, dims) + (dot(ah, bl, dims) + dot(al, bh, dims))


NN = ((1,), (0,))
NT = ((1,), (1,))
TN = ((0,), (0,))


def slots_of(route, rank, plane, column, size, cap):
    own = jnp.right_shift(route, size.bit_length() - 1)
    chip = jnp.bitwise_and(route, size - 1)
    near = jnp.bitwise_xor(own, plane)
    inner = jnp.bitwise_and(jnp.bitwise_xor(jnp.right_shift(own, 1), own), 1)
    step = jnp.where(near < 2, near, 3 - inner)
    mask = jnp.bitwise_xor(chip, column)
    return (step * size + mask) * cap + rank


def position(size):
    at = lax.axis_index("expert")
    return jnp.right_shift(at, size.bit_length() - 1), jnp.bitwise_and(at, size - 1)


def slot_column(size, cap, groups, route):
    count = route.shape[0]
    plane, column = position(size)
    hot = (lax.broadcasted_iota(jnp.int32, (count, groups), 1) == route).astype(F32)
    ahead = (
        lax.broadcasted_iota(jnp.int32, (count, count), 1)
        < lax.broadcasted_iota(jnp.int32, (count, count), 0)
    ).astype(F32).astype(BF16)
    before = dot(ahead, hot.astype(BF16), NN)
    rank = jnp.sum(before * hot, axis=1, keepdims=True).astype(jnp.int32)
    return slots_of(route, rank, plane, column, size, cap)


def pack_body(size, cap, groups, steps, with_column, *refs):
    route_ref, rows_ref, cots_ref = refs[:3]
    outs = refs[3:]
    if with_column:
        outs[-1][...] = slot_column(size, cap, groups, outs[0][...])
        outs = outs[1:-1]
    count, _ = rows_ref.shape
    plane, column = position(size)
    route = route_ref[...]
    hot = (lax.broadcasted_iota(jnp.int32, (groups, count), 0) == route).astype(F32)
    ahead = (
        lax.broadcasted_iota(jnp.int32, (count, count), 0)
        < lax.broadcasted_iota(jnp.int32, (count, count), 1)
    ).astype(F32).astype(BF16)
    before = dot(hot.astype(BF16), ahead, NN)
    rank = jnp.sum(before * hot, axis=0, keepdims=True).astype(jnp.int32)
    slot = slots_of(route, rank, plane, column, size, cap)
    data = [split(rows_ref[...]), split(cots_ref[...])]
    block = size * cap
    for part, step in enumerate(steps):
        pick = (
            lax.broadcasted_iota(jnp.int32, (block, count), 0) + step * block == slot
        ).astype(F32).astype(BF16)
        for kind, (high, low) in enumerate(data):
            rows = dot(pick, high, NN) + dot(pick, low, NN)
            for mask in range(size):
                outs[part * size + mask][kind] = rows[mask * cap : (mask + 1) * cap]


def pack(route_row, rows, cots, size, cap, groups, steps, route_col=None):
    count, width = rows.shape
    with_column = route_col is not None
    column = [pltpu.HBM((count, 1), jnp.int32)] if with_column else []
    rows, cots = (pltpu.with_memory_space_constraint(v, pltpu.HBM) for v in (rows, cots))
    row_spec = pl.BlockSpec((count, width), lambda i: (0, 0))
    out_spec = pl.BlockSpec((2, cap, width), lambda i: (0, 0, 0))
    in_specs = [pl.BlockSpec((1, count), lambda i: (0, 0)), row_spec, row_spec]
    col_spec = pl.BlockSpec((count, 1), lambda i: (0, 0))
    made = pl.pallas_call(
        functools.partial(pack_body, size, cap, groups, steps, with_column),
        grid=(1,),
        in_specs=in_specs + [col_spec] * with_column,
        out_specs=[out_spec] * (len(steps) * size) + [col_spec] * with_column,
        out_shape=[
            (pltpu.HBM if m == 0 else jax.ShapeDtypeStruct)((2, cap, width), F32)
            for m in list(range(size)) * len(steps)
        ]
        + column,
        compiler_params=pltpu.CompilerParams(vmem_limit_bytes=48 * 2**20),
        cost_estimate=pl.CostEstimate(
            flops=8 * count * count * width, bytes_accessed=12 * count * width, transcendentals=0
        ),
        name="pack",
    )(route_row, rows, cots, *([route_col] if with_column else []))
    return [made[i * size : (i + 1) * size] for i in range(len(steps))], made[-1]


def unpack_body(size, cap, steps, added, slot_ref, *refs):
    out_ref = refs[-1]
    count = out_ref.shape[0]
    slot = slot_ref[...]
    total = refs[size][...] if added else None
    for which, step in enumerate(steps):
        rows = jnp.concatenate([refs[m][which] for m in range(size)], axis=0)
        high, low = split(rows)
        at = lax.broadcasted_iota(jnp.int32, (count, size * cap), 1) + step * size * cap
        pick = (at == slot).astype(F32).astype(BF16)
        term = dot(pick, high, NN) + dot(pick, low, NN)
        total = term if total is None else total + term
    out_ref[...] = total


def unpack(slot_col, pieces, before, steps, cap):
    size = len(pieces)
    count = slot_col.shape[0]
    width = pieces[0].shape[-1]
    added = before is not None
    return pl.pallas_call(
        functools.partial(unpack_body, size, cap, steps, added),
        out_shape=jax.ShapeDtypeStruct((count, width), F32),
        compiler_params=pltpu.CompilerParams(vmem_limit_bytes=48 * 2**20),
        cost_estimate=pl.CostEstimate(
            flops=4 * count * count * width, bytes_accessed=12 * count * width, transcendentals=0
        ),
        name="unpack",
    )(slot_col, *pieces, *([before] if added else []))


def adam_body(w_ref, one_ref, two_ref, base_ref, mid_ref, far_ref, *refs):
    new_w, new_one, new_two = refs[-3:]
    grad = base_ref[0] + (mid_ref[0] + far_ref[0])
    one = 0.9 * one_ref[0, 0] + 0.1 * grad
    two = 0.999 * two_ref[0, 0] + 0.001 * grad * grad
    new_one[0, 0] = one
    new_two[0, 0] = two
    new_w[0, 0] = w_ref[0, 0] - 0.01 * (one / CORR_ONE) / (jnp.sqrt(two / CORR_TWO) + 1e-08)


def adam(weights, moment_one, moment_two, base, mid, far, chunk, mid_low, buffers):
    _, _, shard, width = weights.shape
    low = min(chunk)
    whole = pl.BlockSpec((1, 1, shard, width), lambda i: (low + i, 0, 0, 0))
    aliased = buffers is not None
    return pl.pallas_call(
        adam_body,
        grid=(len(chunk),),
        in_specs=[whole] * 3
        + [
            pl.BlockSpec((1, shard, width), lambda i: (low + i, 0, 0)),
            pl.BlockSpec((1, shard, width), lambda i: (low - mid_low + i, 0, 0)),
            pl.BlockSpec((1, shard, width), lambda i: (i, 0, 0)),
        ]
        + [pl.BlockSpec(memory_space=pl.ANY)] * (3 if aliased else 0),
        out_specs=[whole] * 3,
        out_shape=[jax.ShapeDtypeStruct(weights.shape, F32)] * 3,
        input_output_aliases={6 + i: i for i in range(3)} if aliased else {},
        compiler_params=pltpu.CompilerParams(vmem_limit_bytes=48 * 2**20),
        cost_estimate=pl.CostEstimate(
            flops=20 * len(chunk) * shard * width,
            bytes_accessed=36 * len(chunk) * shard * width,
            transcendentals=len(chunk) * shard * width,
        ),
        name="adam",
    )(weights, moment_one, moment_two, base, mid, far, *(buffers or ()))


def step_body(size, cap, layers, chunks, aliased, *refs):
    sent = refs[:size]
    mine, other = refs[size : size + 2]
    at = size + 2 + (size if aliased else 0)
    outs = refs[at : at + size]
    at += size
    keeps = refs[at : at + len(chunks)]
    sends = refs[at + len(chunks) : at + 2 * len(chunks)]
    at += 2 * len(chunks)
    wh, wl, ah, al, slope, full = refs[at:]
    width = full.shape[0]
    shard = mine.shape[1]
    core = lax.axis_index("replica")
    here = pl.multiple_of(core * shard, shard)
    there = pl.multiple_of(width - shard - core * shard, shard)

    for m in range(size):
        high, low = split(sent[m][0])
        ah[0, m * cap : (m + 1) * cap] = high
        al[0, m * cap : (m + 1) * cap] = low

    def weights(layer):
        high, low = split(mine[layer])
        wh[layer, pl.ds(here, shard)] = high
        wl[layer, pl.ds(here, shard)] = low
        high, low = split(other[layer])
        wh[layer, pl.ds(there, shard)] = high
        wl[layer, pl.ds(there, shard)] = low

    def forward(layer, _):
        weights(layer)
        pre = dot3(ah[layer], al[layer], wh[layer], wl[layer], NN)
        sigma = jax.nn.sigmoid(pre)
        high, low = split(pre * sigma)
        ah[layer + 1] = high
        al[layer + 1] = low
        slope[layer] = sigma * (1.0 + pre * (1.0 - sigma))
        return 0

    lax.fori_loop(0, layers - 1, forward, 0)
    last = layers - 1
    weights(last)
    result = dot3(ah[last], al[last], wh[last], wl[last], NN)
    for m in range(size):
        outs[m][0] = result[m * cap : (m + 1) * cap]

    delta = jnp.concatenate([sent[m][1] for m in range(size)], axis=0)
    dh, dl = split(delta)
    for keep, send, chunk in zip(keeps, sends, chunks):
        for layer in chunk:
            place = layer - min(chunk)
            full[...] = dot3(ah[layer], al[layer], dh, dl, TN)
            keep[place] = full[pl.ds(here, shard)]
            send[place] = full[pl.ds(there, shard)]
            if layer > 0:
                back = dot3(dh, dl, wh[layer], wl[layer], NT)
                dh, dl = split(back * slope[layer - 1])


def step_call(sent, mine, other, buffers, which, chunks):
    size = len(sent)
    cap, width = sent[0].shape[1:]
    layers, shard = mine.shape[:2]
    items = size * cap
    row_spec = pl.BlockSpec((2, cap, width), lambda i: (0, 0, 0))
    weight_spec = pl.BlockSpec((layers, shard, width), lambda i: (0, 0, 0))
    outs = [pltpu.HBM((2, cap, width), F32)] * size
    out_specs = [pl.BlockSpec((1, cap, width), lambda i: (which, 0, 0))] * size
    grads = [jax.ShapeDtypeStruct((len(c), shard, width), F32) for c in chunks] * 2
    grad_specs = [pl.BlockSpec((len(c), shard, width), lambda i: (0, 0, 0)) for c in chunks] * 2
    aliased = buffers is not None
    result = pl.pallas_call(
        functools.partial(step_body, size, cap, layers, chunks, aliased),
        grid=(1,),
        in_specs=[row_spec] * size
        + [weight_spec] * 2
        + [pl.BlockSpec(memory_space=pl.ANY)] * (size if aliased else 0),
        out_specs=out_specs + grad_specs,
        out_shape=outs + grads,
        input_output_aliases={size + 2 + m: m for m in range(size)} if aliased else {},
        scratch_shapes=[
            pltpu.VMEM((layers, width, width), BF16),
            pltpu.VMEM((layers, width, width), BF16),
            pltpu.VMEM((layers, items, width), BF16),
            pltpu.VMEM((layers, items, width), BF16),
            pltpu.VMEM((layers - 1, items, width), F32),
            pltpu.VMEM((width, width), F32),
        ],
        compiler_params=pltpu.CompilerParams(vmem_limit_bytes=48 * 2**20),
        cost_estimate=pl.CostEstimate(
            flops=18 * layers * items * width * width,
            bytes_accessed=4 * (3 * items * width + 2 * layers * width * width),
            transcendentals=layers * items * width,
        ),
        name="step",
    )(*sent, mine, other, *(buffers or ()))
    n = len(chunks)
    return result[:size], result[size : size + n], result[size + n :]


PAIRS = ((1, 2), (0, 3))


def chunks_of(layers, step):
    order = list(range(layers - 1, -1, -1))
    first, second = layers // 2, layers - 1 - layers // 2
    cut = [order[:first], order[first : first + second], order[first + second :]]
    return cut if step > 1 else [order]


def on_device(samples, routes, cotangent, weights, moment_one, moment_two):
    count = samples.shape[0]
    groups = lax.axis_size("expert")
    cap = 2 * count // groups
    size = groups // PLANES
    layers = weights.shape[0]
    route_row = routes.reshape(1, count)

    def plane_pairs(pairs):
        return [(a * size + p, b * size + p) for a, b in pairs for p in range(size)]

    def along(value, pairs):
        return lax.ppermute(value, "expert", plane_pairs(pairs))

    def swap_core(value):
        return lax.ppermute(value, "replica", [(0, 1), (1, 0)])

    def exchange(values):
        moved = [values[0]]
        for mask in range(1, size):
            moved.append(
                lax.ppermute(values[mask], "expert", [(e, e ^ mask) for e in range(groups)])
            )
        return moved

    SIDES = [(0, 1), (1, 0), (2, 3), (3, 2)]
    MIDDLE = [(1, 2), (2, 1)]
    OUTWARD = [(1, 0), (2, 3)]
    INWARD = [(0, 1), (3, 2)]
    FAR = [(1, 3), (2, 0)]
    plane, _ = position(size)
    inner = jnp.logical_and(plane > 0, plane < PLANES - 1)

    own = weights[:, 0]
    side = along(own, SIDES)
    middle = along(own, MIDDLE)
    own_other = swap_core(own)
    arrived = {}
    for i, steps in enumerate(PAIRS):
        packed, slot_col = pack(
            route_row, samples, cotangent, size, cap, groups, steps, routes if i else None
        )
        for step, values in zip(steps, packed):
            arrived[step] = exchange(values)
    side_in = along(side, MIDDLE)
    middle_out = along(middle, OUTWARD)
    second = middle + middle_out

    mats = {
        0: lambda: (own, own_other),
        1: lambda: (side, swap_core(side)),
        2: lambda: (second, swap_core(second)),
        3: lambda: (third, swap_core(third)),
    }
    outputs = {}
    sums = {}
    for i, steps in enumerate(PAIRS):
        buffers = None
        for which, step in enumerate(steps):
            if step == 3:
                late, _ = lax.optimization_barrier((p3, buffers[0]))
                third = jnp.where(inner, side_in, late)
            pair = mats[step]()
            buffers, keeps, sends = step_call(
                arrived[step], *pair, buffers, which, chunks_of(layers, step)
            )
            sums[step] = [keep + swap_core(send) for keep, send in zip(keeps, sends)]
            if step == 1:
                one = sums[1][0]
                p3 = along(jnp.where(inner, side_in, one), SIDES)
        outputs[i] = exchange(buffers)

    zero = sums[0][0]
    cut_two, cut_three = chunks_of(layers, 2), chunks_of(layers, 3)
    p4, mid = [], []
    for value, c in zip(sums[2], cut_two):
        back = along(jnp.where(inner, one[min(c) : max(c) + 1], value), SIDES)
        p4.append(back)
        joined = value + back
        mid.append(along(joined, MIDDLE))
    kept, sides, *late = lax.optimization_barrier((zero, p3, *p4))
    base = kept + jnp.where(inner, sides, jnp.concatenate(late[::-1], axis=0))
    updated = None
    for value, c in zip(sums[3], cut_three):
        passed = value + along(value, INWARD)
        far = along(passed, FAR)
        k = next(k for k, d in enumerate(cut_two) if min(c) in d)
        updated = adam(
            weights, moment_one, moment_two, base, mid[k], far, c, min(cut_two[k]), updated
        )
    result = None
    for i, steps in enumerate(PAIRS):
        result = unpack(slot_col, outputs[i], result, steps, cap)
    return (result, *updated)


def solution(mesh):
    placed = (
        P(("expert", "replica"), None),
        P(("expert", "replica"), None),
        P(("expert", "replica"), None),
        P(None, "expert", "replica", None),
        P(None, "expert", "replica", None),
        P(None, "expert", "replica", None),
    )
    return jax.shard_map(
        on_device,
        mesh=mesh,
        in_specs=placed,
        out_specs=(
            P(("expert", "replica"), None),
            P(None, "expert", "replica", None),
            P(None, "expert", "replica", None),
            P(None, "expert", "replica", None),
        ),
        check_vma=False,
    )
```
